512 devices in a mesh: energy: 8 (over y_lo, core), atom: 64 (over y_hi, x, z).
Axes of the slice: x: 4, y: 8 (y_hi: 2, y_lo: 4; y = y_hi * 4 + y_lo), z: 8, core: 2. Of those that a mesh axis runs over, the one named last changes fastest.
Arguments:
- green: bfloat16 [8, 64, 2, 512, 512], P('energy', 'atom'), may hold values from -0.25 to 0.25
- t_ref: bfloat16 [8, 64, 2, 32, 32], P('energy'), may hold values from -0.24748737 to 0.24748737
- radial: bfloat16 [8, 32, 1024], P('energy'), may hold values from -1 to 1
- energy_weight: float32 [8], P('energy'), may hold values from 10 to 60
- potential: float32 [64, 25, 1024], P('atom'), may hold values from -6 to 6
- coupling: float32 [25, 32], replicated, may hold values from -1 to 1
- zone: int32 [64, 15], P('atom'), may hold values from 0 to 63, as said below
- order: int32 [64], replicated, may hold values from 0 to 63, as said below
Outputs:
- mixed: float32 [64, 25, 1024], P('atom')
- final_density: float32 [64, 25, 1024], P('atom')
The draws below stay inside these ranges and needn't reach their ends.
Inputs may be any that keep to these rules, and one draw needn't show every extreme that they name: `zone`: each row lists 16 - 1 distinct atom ids, none of them the atom at that row's position. `order`: A permutation of the atom ids.
All inputs are finite; a program needn't handle non-finite values.
Results may differ from the reference program's by a relative error of at most 0.035.
Values may be sent and summed in bfloat16 or wider, within the bound.
A program may use at most 64 MiB of HBM per device.

```python
import math
import jax
import jax.numpy as jnp
from jax import lax

CH = 32
ZONE = 16
NCHAN = 25
NRAD = 1024
NITER = 4
ATOMS = 64
ENERGIES = 8
ORD = 512


def atom_order(key):
    return jax.random.permutation(jax.random.fold_in(key, 11), ATOMS).astype(jnp.int32)


def member_offsets(row_key):
    return jax.random.permutation(row_key, ATOMS - 1)[:ZONE - 1]


def draw_order(key, part):
    return atom_order(key)


def draw_zone(key, part):
    permuted = atom_order(key)
    row_keys = jax.random.split(jax.random.fold_in(key, 23), ATOMS)
    offsets = jax.vmap(member_offsets)(row_keys) + 1
    row_ids = (jnp.arange(ATOMS, dtype=jnp.int32)[:, None] + offsets.astype(jnp.int32)) % ATOMS
    return permuted[row_ids].astype(jnp.int32)


def bounded_entries(key, shape, spread, limit):
    values = jnp.clip(jax.random.normal(jax.random.fold_in(key, 7), shape, jnp.float32), -limit, limit)
    return values * spread


def draw_green(key, part):
    shape = (ENERGIES, ATOMS, 2, ORD, ORD)
    return bounded_entries(key, shape, (ORD // 2) ** (-0.5), 4.0).astype(jnp.bfloat16)


def draw_t_ref(key, part):
    shape = (ENERGIES, ATOMS, 2, CH, CH)
    return bounded_entries(key, shape, 0.35 * CH ** (-0.5), 4.0).astype(jnp.bfloat16)


def block_scale(key, dims, cuts, smallest, high):
    def one(position, parts):
        draws = jax.random.uniform(jax.random.fold_in(jax.random.fold_in(key, 6), position), (parts,), jnp.float32, smallest / len(cuts), high / len(cuts))
        return jnp.repeat(jnp.exp(draws), dims[position] // parts).reshape((-1,) + (1,) * (len(dims) - position - 1))

    loudness = one(*cuts[0])
    for cut in cuts[1:]:
        loudness = loudness * one(*cut)
    return loudness


def gaussian(stream_key, dims, width, most, cuts=(), kind=jnp.bfloat16):
    array = jax.random.normal(stream_key, dims, jnp.float32) * width
    if len(cuts) > 0:
        array = block_scale(stream_key, dims, cuts, -0.22, 0.18) * array
    return jnp.clip(array, min=-most, max=most).astype(kind)


def setup_inputs(seed: int = 0) -> dict:
    seeds = jax.random.split(jax.random.key(seed), 9)
    green = draw_green(jax.random.fold_in(seeds[8], 71), 0)
    t_ref = draw_t_ref(jax.random.fold_in(seeds[8], 71), 0)
    radial = gaussian(seeds[2], (ENERGIES, CH, NRAD), (NRAD ** -0.25), 1.0, ((0, 8),))
    energy_weight = jnp.clip(jnp.exp(math.log(60.0) - 1.7917595 * jax.random.uniform(seeds[3], (ENERGIES,), jnp.float32) ** block_scale(seeds[3], (ENERGIES,), ((0, 8),), -0.2, 0.2)), 10.0, 60.0)
    potential = gaussian(seeds[4], (ATOMS, NCHAN, NRAD), 1.0, 6.0, ((0, 64),), jnp.float32)
    coupling = gaussian(seeds[5], (NCHAN, CH), CH ** -0.5, 1.0, (), jnp.float32)
    zone = draw_zone(jax.random.fold_in(seeds[8], 71), 0)
    order = draw_order(jax.random.fold_in(seeds[8], 71), 0)
    return dict(green=green, t_ref=t_ref, radial=radial, energy_weight=energy_weight, potential=potential, coupling=coupling, zone=zone, order=order)


MIXING = 0.5
STEEPNESS = 0.8


def rounded(values):
    return lax.optimization_barrier(values.astype(jnp.bfloat16)).astype(jnp.float32)


def rebuild(field, basis, coupling, t_base):
    squares = basis.astype(jnp.float32) ** 2
    intersection = jnp.einsum('acr,br->acb', field, squares, precision=lax.Precision.HIGHEST)
    drive = jnp.einsum('acb,cb->ab', intersection, coupling, precision=lax.Precision.HIGHEST)
    scale = 1.0 + STEEPNESS * jnp.tanh(drive)
    return (scale[:, None, :, None] * t_base.astype(jnp.float32)).astype(jnp.bfloat16)


def scatter(zone_t, greens, channels):
    count = zone_t.shape[0]
    zone_size = zone_t.shape[1]
    order_size = zone_size * channels
    tmat = zone_t.astype(jnp.float32)
    seed_block = jnp.concatenate([tmat[:, 0, 0], tmat[:, 0, 1]], -1)
    start = jnp.zeros((count, zone_size, channels, 2 * channels), jnp.float32).at[:, 0].set(seed_block)
    stacked = greens.astype(jnp.float32).reshape(count, 2 * order_size, order_size)
    iterate = start
    for sweep in range(NITER):
        current = rounded(iterate).reshape(count, order_size, 2 * channels)
        product = jnp.einsum('aij,ajk->aik', stacked, current).reshape(count, 2, zone_size, channels, 2 * channels)
        real_part = product[:, 0, :, :, :channels] - product[:, 1, :, :, channels:]
        imag_part = product[:, 0, :, :, channels:] + product[:, 1, :, :, :channels]
        scattered = rounded(jnp.concatenate([real_part, imag_part], -1))
        left = jnp.einsum('azbc,azcd->azbd', tmat[:, :, 0], scattered)
        right = jnp.einsum('azbc,azcd->azbd', tmat[:, :, 1], scattered)
        update = jnp.concatenate([left[..., :channels] - right[..., channels:], left[..., channels:] + right[..., :channels]], -1)
        iterate = start + update
    return iterate[:, 0, :, channels:]


def density(imag_tau, basis, coupling, weight):
    radial_f = basis.astype(jnp.float32)
    mixed_rows = jnp.einsum('aij,jr->air', imag_tau, radial_f, precision=lax.Precision.HIGHEST)
    paired = radial_f[None] * mixed_rows
    return weight * jnp.einsum('ci,air->acr', coupling, paired, precision=lax.Precision.HIGHEST)


def reference(green, t_ref, radial, energy_weight, potential, coupling, zone, order):
    channels = coupling.shape[1]
    index_list = jnp.arange(ATOMS, dtype=jnp.int32)
    position_of = jnp.zeros((ATOMS,), jnp.int32).at[order].set(index_list)
    zone_pos = jnp.concatenate([index_list[:, None], position_of[zone]], 1)

    def one_pass(field):
        def per_energy(energy_idx):
            t_all = rebuild(field, radial[energy_idx], coupling, t_ref[energy_idx])
            imag_tau = scatter(t_all[zone_pos], green[energy_idx], channels)
            return density(imag_tau, radial[energy_idx], coupling, energy_weight[energy_idx])
        return jnp.sum(lax.map(per_energy, jnp.arange(ENERGIES, dtype=jnp.int32)), axis=0)

    first = one_pass(potential)
    mixed = (1.0 - MIXING) * potential + MIXING * first
    return mixed, one_pass(mixed)
```

```python
import functools

import jax
import jax.numpy as jnp
from jax import lax
from jax.experimental import pallas as pl
from jax.experimental.pallas import tpu as pltpu
from jax.sharding import PartitionSpec as P

MIXING = 0.5
STEEPNESS = 0.8
F32 = jnp.float32
BF16 = jnp.bfloat16
MESH = pl.DeviceIdType.MESH
NT = (((1,), (1,)), ((), ()))
NN = (((1,), (0,)), ((), ()))
TN = (((0,), (0,)), ((), ()))


def dot(left, right, dims=NN):
    return lax.dot_general(left, right, dims, preferred_element_type=F32)


def split(values):
    high = values.astype(BF16)
    return high, (values - high.astype(F32)).astype(BF16)


def scale_of(drive):
    return 1.0 + STEEPNESS * jnp.tanh(drive)


def kernel(
    energies, atoms, members,
    green, t_ref, radial, weight, potential, coupling, zone, order,
    mixed, final,
    g_v, t_v, rad_v, v_v, w_v, high4, low4, drives, scales_a, scales_b, tau1, tau2, mixed_v, final_v,
    local_sem, drive_send, drive_recv, scale_send, scale_recv, tau_send, tau_recv,
    rad_send, rad_recv, fwd_send, fwd_recv,
):
    channels = radial.shape[1]
    size = members * channels
    plane = atoms // 2
    depth = 8
    width = plane // depth
    me_e = lax.axis_index("energy")
    me_a = lax.axis_index("atom")
    half = me_a // plane
    spot = me_a % plane
    here_x, here_z = spot // depth, spot % depth
    weight_value = weight[0]

    own_rows = pl.ds(pl.multiple_of(me_e * channels, channels), channels)
    loads = [
        pltpu.make_async_copy(potential.at[0], v_v, local_sem.at[0]),
        pltpu.make_async_copy(radial.at[0], rad_v.at[own_rows], local_sem.at[1]),
        pltpu.make_async_copy(t_ref.at[0], t_v, local_sem.at[2]),
        pltpu.make_async_copy(green.at[0, 0], g_v, local_sem.at[3]),
    ]
    for load in loads:
        load.start()

    offsets = [(dx, dz) for dx in range(width) for dz in range(depth) if (dx, dz) != (0, 0)]
    offsets.sort(key=lambda d: -(min(d[0], width - d[0]) + min(d[1], depth - d[1])))

    def plane_peer(offset):
        x, z = (here_x + offset[0]) % width, (here_z + offset[1]) % depth
        return (me_e, half * plane + x * depth + z)

    def line_peer(other_half, offset):
        side = (half + 1) % 2 if other_half else half
        return ((me_e + offset) % energies, side * plane + spot)

    line = [(h, o) for h in (1, 0) for o in range(energies) if (h, o) != (0, 0)]
    barrier = pltpu.get_barrier_semaphore()
    for offset in offsets:
        pl.semaphore_signal(barrier, inc=1, device_id=plane_peer(offset), device_id_type=MESH)
    for h, o in line:
        pl.semaphore_signal(barrier, inc=1, device_id=line_peer(h, o), device_id_type=MESH)

    wanted = [zone[0, k] for k in range(members - 1)]

    def look(j, found):
        atom = order[j]
        return tuple(jnp.where(atom == w, j, f) for w, f in zip(wanted, found))

    found = lax.fori_loop(0, atoms, look, tuple(jnp.int32(0) for _ in wanted))
    positions = [me_a] + list(found)
    slots = [2 * (p % plane) + p // plane for p in positions]

    lane_block = lax.broadcasted_iota(jnp.int32, (1, 128), 1) // channels
    copies = 128 // channels

    loads[0].wait()
    loads[1].wait()
    basis = rad_v[own_rows, :].astype(F32)
    high, low = split(basis * basis)
    high4[...] = jnp.concatenate([high] * copies, 0)
    low4[...] = jnp.concatenate([low] * copies, 0)
    coup = coupling[...]
    coup4 = jnp.concatenate([coup] * copies, 1)
    v_high, v_low = split(v_v[...])
    inter = (
        dot(v_high, high4[...], NT) + dot(v_high, low4[...], NT)
        + dot(v_low, high4[...], NT) + dot(v_low, low4[...], NT)
    )
    drives[half] = jnp.sum(inter * coup4, axis=0, keepdims=True)

    pl.semaphore_wait(barrier, len(offsets) + len(line))

    drive_copy = pltpu.make_async_remote_copy(
        src_ref=drives.at[half], dst_ref=drives.at[half],
        send_sem=drive_send, recv_sem=drive_recv,
        device_id=line_peer(1, 0), device_id_type=MESH,
    )
    drive_copy.start()

    def rows_of(energy):
        return rad_v.at[pl.ds(pl.multiple_of(energy * channels, channels), channels)]

    partner = (me_e + 1 - 2 * (me_e % 2), me_a)

    def forward(k):
        source = rows_of((me_e + energies - 2 * k) % energies)
        return pltpu.make_async_remote_copy(
            src_ref=source, dst_ref=source, send_sem=fwd_send.at[k], recv_sem=fwd_recv.at[k],
            device_id=partner, device_id_type=MESH,
        )

    def across(k):
        return pltpu.make_async_remote_copy(
            src_ref=rows_of(me_e), dst_ref=rows_of(me_e), send_sem=rad_send.at[k], recv_sem=rad_recv.at[k],
            device_id=((me_e + 2 * k) % energies, me_a), device_id_type=MESH,
        )

    chips = energies // 2
    for k in range(1, chips):
        across(k).start()
    forward(0).start()

    drive_copy.wait_recv()

    scales = (scales_a, scales_b)

    def share(step, rows):
        for h in range(2):
            scales[step][2 * spot + h] = rows[h]
        block = scales[step].at[pl.ds(2 * spot, 2)]
        for offset in offsets:
            pltpu.make_async_remote_copy(
                src_ref=block, dst_ref=block, send_sem=scale_send.at[step], recv_sem=scale_recv.at[step],
                device_id=plane_peer(offset), device_id_type=MESH,
            ).start()

    def shared(step, sem):
        block = scales[step].at[pl.ds(0, 2 * len(offsets))]
        pltpu.make_async_copy(block, block, sem.at[step]).wait()

    first_drives = [drives[h] for h in range(2)]
    share(0, [scale_of(d) for d in first_drives])

    loads[2].wait()
    loads[3].wait()
    for k in range(members):
        t_k = t_v[positions[k]]
        t_both = jnp.concatenate([t_k[0], t_k[1]], 0)
        rows = slice(k * channels, (k + 1) * channels)
        by_real = dot(t_both, g_v[0, rows, :])
        by_imag = dot(t_both, g_v[1, rows, :])
        w_v[rows, :size] = (by_real[:channels] - by_imag[channels:]).astype(BF16)
        w_v[rows, size:] = (by_imag[:channels] + by_real[channels:]).astype(BF16)

    own_t = t_v[me_a].astype(F32)
    seed = jnp.concatenate([own_t[0].T, own_t[1].T], 0)
    seed = jnp.concatenate([seed, jnp.zeros((2 * channels, 128 - channels), F32)], 1)
    seed_all = jnp.concatenate([seed, jnp.zeros((2 * channels, size - 128), F32)], 1)
    imag4 = jnp.concatenate([own_t[1]] * copies, 1)
    square = jnp.concatenate([coup, jnp.zeros((32 - coup.shape[0], channels), F32)], 0)
    square4 = jnp.concatenate([square] * copies, 1)
    cross4 = lax.dot_general(square, square4, TN, preferred_element_type=F32, precision=lax.Precision.HIGHEST)
    c_high, c_low = split(coup)
    diagonal = lax.broadcasted_iota(jnp.int32, (channels, 128), 0) == lax.broadcasted_iota(jnp.int32, (channels, 128), 1)

    def turned(x):
        return jnp.concatenate([-x[channels:], x[:channels]], 0)

    def scatter(step):
        pieces = []
        for v in range(members // copies):
            piece = scales[step][slots[copies * v]]
            for q in range(1, copies):
                piece = jnp.where(lane_block == q, scales[step][slots[copies * v + q]], piece)
            pieces.append(piece)
        rows = jnp.concatenate(pieces, 1)
        own = jnp.sum(jnp.where(diagonal, pieces[0], 0.0), axis=1, keepdims=True) * weight_value
        x = (pieces[0] * seed).astype(BF16)
        y = dot(x, w_v[:, :128], NT) + dot(turned(x), w_v[:, size:size + 128], NT)
        x = (rows * (seed_all + y)).astype(BF16)
        for _ in range(2):
            y = dot(x, w_v[:, :size], NT) + dot(turned(x), w_v[:, size:], NT)
            x = (rows * (seed_all + y)).astype(BF16)
        y = (
            dot(w_v[:channels, :size], jnp.concatenate([x[channels:]] * copies, 0), NT)
            + dot(w_v[:channels, size:], jnp.concatenate([x[:channels]] * copies, 0), NT)
        )
        return own * (imag4 + y)

    def pack(tau):
        rows = channels // copies
        packed = tau[:rows]
        for q in range(1, copies):
            packed = jnp.where(lane_block == q, tau[q * rows:(q + 1) * rows], packed)
        return packed.astype(BF16)

    def spread(tau, r):
        tau = tau.astype(F32)
        rows = []
        for q in range(copies):
            shift = (channels * (r - q)) % 128
            moved = tau if shift == 0 else pltpu.roll(tau, shift, 1)
            rows.append(jnp.where(lane_block == r, moved, 0.0))
        return jnp.concatenate(rows, 0).astype(BF16)

    def paired(sets):
        groups = energies // copies
        blocks = [
            jnp.concatenate([spread(taus(g * copies + r), r) for taus in sets for r in range(copies)], 0)
            for g in range(groups)
        ]
        parts = [[] for _ in sets]
        chunk = 256
        for n in range(0, rad_v.shape[1], chunk):
            sums = [None for _ in sets]
            for g in range(groups):
                base = rad_v[g * 128:(g + 1) * 128, n:n + chunk]
                product = dot(blocks[g], base)
                base = base.astype(F32)
                for s in range(len(sets)):
                    for r in range(copies):
                        at = s * 128 + r * channels
                        term = base[r * channels:(r + 1) * channels] * product[at:at + channels]
                        sums[s] = term if sums[s] is None else sums[s] + term
            for s in range(len(sets)):
                parts[s].append(sums[s])
        return [jnp.concatenate(p, 1) for p in parts]

    def density(high_pair, low_pair):
        return dot(c_high, high_pair) + dot(c_high, low_pair) + dot(c_low, high_pair)

    shared(0, scale_recv)
    mine = half * energies + me_e
    tau1[mine] = pack(scatter(0))
    for h, o in line:
        pltpu.make_async_remote_copy(
            src_ref=tau1.at[mine], dst_ref=tau1.at[mine], send_sem=tau_send.at[0], recv_sem=tau_recv.at[0],
            device_id=line_peer(h, o), device_id_type=MESH,
        ).start()
    for k in range(1, chips):
        across(k).wait_recv()
        forward(k).start()
    for k in range(chips):
        forward(k).wait_recv()
    everyone = tau1.at[pl.ds(0, len(line))]
    pltpu.make_async_copy(everyone, everyone, tau_recv.at[0]).wait()

    pairs = paired([lambda n: tau1[n], lambda n: tau1[energies + n]])
    highs, lows = zip(*[split(p) for p in pairs])
    stacked = jnp.concatenate(list(highs) + list(lows), 0)
    inter = dot(stacked, high4[...], NT) + dot(stacked, low4[...], NT)
    rows = []
    for h in range(2):
        both = inter[h * channels:(h + 1) * channels] + inter[(h + 2) * channels:(h + 3) * channels]
        change = jnp.sum(both * cross4, axis=0, keepdims=True)
        rows.append(scale_of((1.0 - MIXING) * first_drives[h] + MIXING * change))
    share(1, rows)

    own_high = jnp.where(half == 0, highs[0].astype(F32), highs[1].astype(F32)).astype(BF16)
    own_low = jnp.where(half == 0, lows[0].astype(F32), lows[1].astype(F32)).astype(BF16)
    mixed_v[...] = (1.0 - MIXING) * v_v[...] + MIXING * density(own_high, own_low)
    mixed_copy = pltpu.make_async_copy(mixed_v, mixed.at[0], local_sem.at[0])
    mixed_copy.start()

    shared(1, scale_recv)
    tau2[me_e] = pack(scatter(1))
    for o in range(1, energies):
        pltpu.make_async_remote_copy(
            src_ref=tau2.at[me_e], dst_ref=tau2.at[me_e], send_sem=tau_send.at[1], recv_sem=tau_recv.at[1],
            device_id=line_peer(0, o), device_id_type=MESH,
        ).start()

    drive_copy.wait_send()
    for k in range(1, chips):
        across(k).wait_send()
    for k in range(chips):
        forward(k).wait_send()
    shared(0, scale_send)
    shared(1, scale_send)
    pltpu.make_async_copy(everyone, everyone, tau_send.at[0]).wait()
    mixed_copy.wait()

    others = tau2.at[pl.ds(0, energies - 1)]
    pltpu.make_async_copy(others, others, tau_recv.at[1]).wait()
    last = paired([lambda n: tau2[n]])[0]
    final_v[...] = density(*split(last))
    final_copy = pltpu.make_async_copy(final_v, final.at[0], local_sem.at[1])
    final_copy.start()
    pltpu.make_async_copy(others, others, tau_send.at[1]).wait()
    final_copy.wait()


def solution(mesh):
    energies, atoms = mesh.shape["energy"], mesh.shape["atom"]

    def body(green, t_ref, radial, energy_weight, potential, coupling, zone, order):
        members = zone.shape[1] + 1
        channels = coupling.shape[1]
        _, nchan, radii = potential.shape
        size = members * channels
        anywhere = pl.BlockSpec(memory_space=pl.ANY)
        scalars = pl.BlockSpec(memory_space=pltpu.SMEM)
        vectors = pl.BlockSpec(memory_space=pltpu.VMEM)
        dma = pltpu.SemaphoreType.DMA
        out = jax.ShapeDtypeStruct(potential.shape, F32)
        return pl.pallas_call(
            functools.partial(kernel, energies, atoms, members),
            out_shape=(out, out),
            in_specs=[anywhere, anywhere, anywhere, scalars, anywhere, vectors, scalars, scalars],
            out_specs=(anywhere, anywhere),
            scratch_shapes=[
                pltpu.VMEM(green.shape[2:], BF16),
                pltpu.VMEM(t_ref.shape[1:], BF16),
                pltpu.VMEM((energies * channels, radii), BF16),
                pltpu.VMEM((nchan, radii), F32),
                pltpu.VMEM((size, 2 * size), BF16),
                pltpu.VMEM((128, radii), BF16),
                pltpu.VMEM((128, radii), BF16),
                pltpu.VMEM((2, 1, 128), F32),
                pltpu.VMEM((atoms, 1, 128), F32),
                pltpu.VMEM((atoms, 1, 128), F32),
                pltpu.VMEM((2 * energies, 8, 128), BF16),
                pltpu.VMEM((energies, 8, 128), BF16),
                pltpu.VMEM((nchan, radii), F32),
                pltpu.VMEM((nchan, radii), F32),
                dma((4,)), dma, dma, dma((2,)), dma((2,)), dma((2,)), dma((2,)),
                dma((energies // 2,)), dma((energies // 2,)), dma((energies // 2,)), dma((energies // 2,)),
            ],
            compiler_params=pltpu.CompilerParams(collective_id=0, has_side_effects=True),
        )(green, t_ref, radial, energy_weight, potential, coupling, zone, order)

    placed = (
        P("energy", "atom", None, None, None),
        P("energy", None, None, None, None),
        P("energy", None, None),
        P("energy"),
        P("atom", None, None),
        P(),
        P("atom", None),
        P(),
    )
    return jax.shard_map(
        body,
        mesh=mesh,
        in_specs=placed,
        out_specs=(P("atom", None, None), P("atom", None, None)),
        check_vma=False,
    )
```

```python
import functools

import jax
import jax.numpy as jnp
from jax import lax
from jax.experimental import pallas as pl
from jax.experimental.pallas import tpu as pltpu
from jax.sharding import PartitionSpec as P

MIXING = 0.5
STEEPNESS = 0.8
F32 = jnp.float32
BF16 = jnp.bfloat16
MESH = pl.DeviceIdType.MESH
NT = (((1,), (1,)), ((), ()))
NN = (((1,), (0,)), ((), ()))
TN = (((0,), (0,)), ((), ()))


def dot(left, right, dims=NN):
    return lax.dot_general(left, right, dims, preferred_element_type=F32)


def split(values):
    high = values.astype(BF16)
    return high, (values - high.astype(F32)).astype(BF16)


def scale_of(drive):
    return 1.0 + STEEPNESS * jnp.tanh(drive)


def kernel(
    energies, atoms, members,
    green, t_ref, radial, weight, potential, coupling_in, zone_in, order_in,
    both_out,
    g_v, t_v, rad_v, v_v, w_v, high4, low4, drives, scales_a, scales_b, tau1, tau2, own_pair,
    picked, coupling, zone, order,
    local_sem, drive_send, drive_recv, scale_send, scale_recv, tau_send, tau_recv,
    rad_send, rad_recv, fwd_send, fwd_recv,
):
    channels = radial.shape[1]
    size = members * channels
    plane = atoms // 2
    depth = 8
    width = plane // depth
    me_e = lax.axis_index("energy")
    me_a = lax.axis_index("atom")
    half = me_a // plane
    spot = me_a % plane
    here_x, here_z = spot // depth, spot % depth

    own_rows = pl.ds(pl.multiple_of(me_e * channels, channels), channels)
    loads = [
        pltpu.make_async_copy(potential, v_v.at[pl.ds(0, potential.shape[0])], local_sem.at[0]),
        pltpu.make_async_copy(radial.at[0], rad_v.at[own_rows], local_sem.at[1]),
        pltpu.make_async_copy(coupling_in, coupling, local_sem.at[4]),
        pltpu.make_async_copy(t_ref, t_v, local_sem.at[2]),
        pltpu.make_async_copy(green.at[0, 0], g_v, local_sem.at[3]),
        pltpu.make_async_copy(zone_in, zone, local_sem.at[5]),
        pltpu.make_async_copy(order_in, order, local_sem.at[6]),
    ]
    for load in loads:
        load.start()

    offsets = [(dx, dz) for dx in range(width) for dz in range(depth) if (dx, dz) != (0, 0)]
    offsets.sort(key=lambda d: -(min(d[0], width - d[0]) + min(d[1], depth - d[1])))

    def plane_peer(offset):
        x, z = (here_x + offset[0]) % width, (here_z + offset[1]) % depth
        return (me_e, half * plane + x * depth + z)

    def line_peer(other_half, offset):
        side = (half + 1) % 2 if other_half else half
        return ((me_e + offset) % energies, side * plane + spot)

    line = [(h, o) for h in (1, 0) for o in range(energies) if (h, o) != (0, 0)]
    barrier = pltpu.get_barrier_semaphore()
    for offset in offsets:
        pl.semaphore_signal(barrier, inc=1, device_id=plane_peer(offset), device_id_type=MESH)
    for h, o in line:
        pl.semaphore_signal(barrier, inc=1, device_id=line_peer(h, o), device_id_type=MESH)

    lane_block = lax.broadcasted_iota(jnp.int32, (1, 128), 1) // channels
    copies = 128 // channels
    parity = lane_block % 2

    nchan = coupling.shape[0]
    chunks = radial.shape[2] // 128
    whole = nchan // 8 * 8

    def unfolded(ref):
        return jnp.concatenate([ref[pl.ds(j, nchan, stride=chunks), :] for j in range(chunks)], 1)

    def fold(base, value):
        ref = both_out
        for j in range(chunks):
            piece = value[:, j * 128:(j + 1) * 128]
            ref[pl.ds(base + j, whole, stride=chunks), :] = piece[:whole]
            for c in range(whole, nchan):
                at = base + c * chunks + j
                ref[at:at + 1, :] = piece[c:c + 1]

    for load in loads[:3]:
        load.wait()
    basis = rad_v[own_rows, :].astype(F32)
    high, low = split(basis * basis)
    high4[...] = jnp.concatenate([high] * copies, 0)
    low4[...] = jnp.concatenate([low] * copies, 0)
    coup = coupling[...]
    coup4 = jnp.concatenate([coup] * copies, 1)
    v_high, v_low = split(unfolded(v_v))
    inter = (
        dot(v_high, high4[...], NT) + dot(v_high, low4[...], NT)
        + dot(v_low, high4[...], NT) + dot(v_low, low4[...], NT)
    )
    drives[half] = jnp.sum(inter * coup4, axis=0, keepdims=True)

    pl.semaphore_wait(barrier, len(offsets) + len(line))

    drive_copy = pltpu.make_async_remote_copy(
        src_ref=drives.at[half], dst_ref=drives.at[half],
        send_sem=drive_send, recv_sem=drive_recv,
        device_id=line_peer(1, 0), device_id_type=MESH,
    )
    drive_copy.start()

    def rows_of(energy):
        return rad_v.at[pl.ds(pl.multiple_of(energy * channels, channels), channels)]

    partner = (me_e + 1 - 2 * (me_e % 2), me_a)

    def forward(k):
        source = rows_of((me_e + energies - 2 * k) % energies)
        return pltpu.make_async_remote_copy(
            src_ref=source, dst_ref=source, send_sem=fwd_send.at[k], recv_sem=fwd_recv.at[k],
            device_id=partner, device_id_type=MESH,
        )

    def across(k):
        return pltpu.make_async_remote_copy(
            src_ref=rows_of(me_e), dst_ref=rows_of(me_e), send_sem=rad_send.at[k], recv_sem=rad_recv.at[k],
            device_id=((me_e + 2 * k) % energies, me_a), device_id_type=MESH,
        )

    chips = energies // 2
    drive_copy.wait_recv()

    scales = (scales_a, scales_b)

    def share(step, rows):
        scales[step][spot] = jnp.where(parity == 0, rows[0], rows[1])
        block = scales[step].at[pl.ds(spot, 1)]
        for offset in offsets:
            pltpu.make_async_remote_copy(
                src_ref=block, dst_ref=block, send_sem=scale_send.at[step], recv_sem=scale_recv.at[step],
                device_id=plane_peer(offset), device_id_type=MESH,
            ).start()

    def shared(step, sem):
        block = scales[step].at[pl.ds(0, len(offsets))]
        pltpu.make_async_copy(block, block, sem.at[step]).wait()

    first_drives = [drives[h] for h in range(2)]
    share(0, [scale_of(d) for d in first_drives])
    for k in range(1, chips):
        across(k).start()
    forward(0).start()

    for load in loads[3:]:
        load.wait()
    wanted = [zone[0, k] for k in range(members - 1)]

    def look(j, found):
        atom = order[j]
        return tuple(jnp.where(atom == w, j, f) for w, f in zip(wanted, found))

    found = lax.fori_loop(0, atoms, look, tuple(jnp.int32(0) for _ in wanted))
    positions = [me_a] + list(found)
    spots = [p % plane for p in positions]
    sides = [p // plane for p in positions]

    member = lax.broadcasted_iota(jnp.int32, (members, atoms), 0)
    wanted_at = jnp.full((members, atoms), me_a, jnp.int32)
    for k in range(1, members):
        wanted_at = jnp.where(member == k, positions[k], wanted_at)
    one_hot = (lax.broadcasted_iota(jnp.int32, (members, atoms), 1) == wanted_at).astype(F32).astype(BF16)
    planes = 2 * channels
    for n in range(planes // copies):
        block = dot(one_hot, t_v[n * 128:(n + 1) * 128, :], NT)
        for q in range(copies):
            moved = block if q == 0 else pltpu.roll(block, 128 - channels * q, 1)
            picked[pl.ds(n * copies + q, members, stride=planes), :] = moved
    for k in range(members):
        t_both = picked[k * planes:(k + 1) * planes, :channels].astype(BF16)
        rows = slice(k * channels, (k + 1) * channels)
        by_real = dot(t_both, g_v[0, rows, :])
        by_imag = dot(t_both, g_v[1, rows, :])
        w_v[rows, :size] = (by_real[:channels] - by_imag[channels:]).astype(BF16)
        w_v[rows, size:] = (by_imag[:channels] + by_real[channels:]).astype(BF16)

    own_t = [picked[:channels, :channels], picked[channels:planes, :channels]]
    seed = jnp.concatenate([own_t[0].T, own_t[1].T], 0)
    seed = jnp.concatenate([seed, jnp.zeros((2 * channels, 128 - channels), F32)], 1)
    seed_all = jnp.concatenate([seed, jnp.zeros((2 * channels, size - 128), F32)], 1)
    imag4 = jnp.concatenate([own_t[1]] * copies, 1)
    square = jnp.concatenate([coup, jnp.zeros((32 - coup.shape[0], channels), F32)], 0)
    square4 = jnp.concatenate([square] * copies, 1)
    cross4 = lax.dot_general(square, square4, TN, preferred_element_type=F32, precision=lax.Precision.HIGHEST)
    c_high, c_low = split(coup)
    diagonal = lax.broadcasted_iota(jnp.int32, (channels, 128), 0) == lax.broadcasted_iota(jnp.int32, (channels, 128), 1)

    def turned(x):
        return jnp.concatenate([-x[channels:], x[:channels]], 0)

    weight_value = weight[0]

    def scatter(step):
        def row_of(k):
            both = scales[step][spots[k]]
            return jnp.where(parity == sides[k], both, pltpu.roll(both, channels, 1))

        pieces = []
        for v in range(members // copies):
            piece = row_of(copies * v)
            for q in range(1, copies):
                piece = jnp.where(lane_block == q, row_of(copies * v + q), piece)
            pieces.append(piece)
        rows = jnp.concatenate(pieces, 1)
        own = jnp.sum(jnp.where(diagonal, pieces[0], 0.0), axis=1, keepdims=True) * weight_value
        x = (pieces[0] * seed).astype(BF16)
        y = dot(x, w_v[:, :128], NT) + dot(turned(x), w_v[:, size:size + 128], NT)
        x = (rows * (seed_all + y)).astype(BF16)
        for _ in range(2):
            y = dot(x, w_v[:, :size], NT) + dot(turned(x), w_v[:, size:], NT)
            x = (rows * (seed_all + y)).astype(BF16)
        y = (
            dot(w_v[:channels, :size], jnp.concatenate([x[channels:]] * copies, 0), NT)
            + dot(w_v[:channels, size:], jnp.concatenate([x[:channels]] * copies, 0), NT)
        )
        return own * (imag4 + y)

    def pack(tau):
        rows = channels // copies
        packed = tau[:rows]
        for q in range(1, copies):
            packed = jnp.where(lane_block == q, tau[q * rows:(q + 1) * rows], packed)
        return packed.astype(BF16)

    def spread(tau, r):
        tau = tau.astype(F32)
        rows = []
        for q in range(copies):
            shift = (channels * (r - q)) % 128
            moved = tau if shift == 0 else pltpu.roll(tau, shift, 1)
            rows.append(jnp.where(lane_block == r, moved, 0.0))
        return jnp.concatenate(rows, 0).astype(BF16)

    def paired(sets):
        groups = energies // copies
        blocks = [
            jnp.concatenate([spread(taus(g * copies + r), r) for taus in sets for r in range(copies)], 0)
            for g in range(groups)
        ]
        parts = [[] for _ in sets]
        chunk = 256
        for n in range(0, rad_v.shape[1], chunk):
            sums = [None for _ in sets]
            for g in range(groups):
                base = rad_v[g * 128:(g + 1) * 128, n:n + chunk]
                product = dot(blocks[g], base)
                base = base.astype(F32)
                for s in range(len(sets)):
                    for r in range(copies):
                        at = s * 128 + r * channels
                        term = base[r * channels:(r + 1) * channels] * product[at:at + channels]
                        sums[s] = term if sums[s] is None else sums[s] + term
            for s in range(len(sets)):
                parts[s].append(sums[s])
        return [jnp.concatenate(p, 1) for p in parts]

    def density(high_pair, low_pair):
        return dot(c_high, high_pair) + dot(c_high, low_pair) + dot(c_low, high_pair)

    shared(0, scale_recv)
    mine = half * energies + me_e
    tau1[mine] = pack(scatter(0))
    for h, o in line:
        pltpu.make_async_remote_copy(
            src_ref=tau1.at[mine], dst_ref=tau1.at[mine], send_sem=tau_send.at[0], recv_sem=tau_recv.at[0],
            device_id=line_peer(h, o), device_id_type=MESH,
        ).start()
    for k in range(1, chips):
        across(k).wait_recv()
        forward(k).start()
    for k in range(chips):
        forward(k).wait_recv()
    everyone = tau1.at[pl.ds(0, len(line))]
    pltpu.make_async_copy(everyone, everyone, tau_recv.at[0]).wait()

    pairs = paired([lambda n: tau1[n], lambda n: tau1[energies + n]])
    highs, lows = zip(*[split(p) for p in pairs])
    stacked = jnp.concatenate(list(highs) + list(lows), 0)
    inter = dot(stacked, high4[...], NT) + dot(stacked, low4[...], NT)
    rows = []
    for h in range(2):
        both = inter[h * channels:(h + 1) * channels] + inter[(h + 2) * channels:(h + 3) * channels]
        change = jnp.sum(both * cross4, axis=0, keepdims=True)
        rows.append(scale_of((1.0 - MIXING) * first_drives[h] + MIXING * change))
    share(1, rows)

    for n, parts in enumerate((highs, lows)):
        own_pair[n] = jnp.where(half == 0, parts[0].astype(F32), parts[1].astype(F32)).astype(BF16)

    shared(1, scale_recv)
    tau2[me_e] = pack(scatter(1))
    for o in range(1, energies):
        pltpu.make_async_remote_copy(
            src_ref=tau2.at[me_e], dst_ref=tau2.at[me_e], send_sem=tau_send.at[1], recv_sem=tau_recv.at[1],
            device_id=line_peer(0, o), device_id_type=MESH,
        ).start()

    fold(0, (1.0 - MIXING) * unfolded(v_v) + MIXING * density(own_pair[0], own_pair[1]))

    drive_copy.wait_send()
    for k in range(1, chips):
        across(k).wait_send()
    for k in range(chips):
        forward(k).wait_send()
    shared(0, scale_send)
    shared(1, scale_send)
    pltpu.make_async_copy(everyone, everyone, tau_send.at[0]).wait()

    others = tau2.at[pl.ds(0, energies - 1)]
    pltpu.make_async_copy(others, others, tau_recv.at[1]).wait()
    last = paired([lambda n: tau2[n]])[0]
    fold(nchan * chunks, density(*split(last)))
    pltpu.make_async_copy(others, others, tau_send.at[1]).wait()


def solution(mesh):
    energies, atoms = mesh.shape["energy"], mesh.shape["atom"]

    def body(green, t_ref, radial, energy_weight, potential, coupling, zone, order):
        members = zone.shape[1] + 1
        channels = coupling.shape[1]
        _, nchan, radii = potential.shape
        size = members * channels
        anywhere = pl.BlockSpec(memory_space=pl.ANY)
        vectors = pl.BlockSpec(memory_space=pltpu.VMEM)
        scalars = pl.BlockSpec(memory_space=pltpu.SMEM)
        dma = pltpu.SemaphoreType.DMA
        folded = nchan * radii // 128
        padded = -(-nchan // 8) * 8 * radii // 128
        out = pltpu.VMEM((2 * folded, 128), F32)
        atoms_last = t_ref.transpose(0, 2, 3, 4, 1).reshape(2 * channels * channels, atoms)
        both = pl.pallas_call(
            functools.partial(kernel, energies, atoms, members),
            out_shape=out,
            in_specs=[anywhere, anywhere, anywhere, scalars, anywhere, anywhere, anywhere, anywhere],
            out_specs=vectors,
            scratch_shapes=[
                pltpu.VMEM(green.shape[2:], BF16),
                pltpu.VMEM(atoms_last.shape, BF16),
                pltpu.VMEM((energies * channels, radii), BF16),
                pltpu.VMEM((padded, 128), F32),
                pltpu.VMEM((size, 2 * size), BF16),
                pltpu.VMEM((128, radii), BF16),
                pltpu.VMEM((128, radii), BF16),
                pltpu.VMEM((2, 1, 128), F32),
                pltpu.VMEM((atoms // 2, 1, 128), F32),
                pltpu.VMEM((atoms // 2, 1, 128), F32),
                pltpu.VMEM((2 * energies, 8, 128), BF16),
                pltpu.VMEM((energies, 8, 128), BF16),
                pltpu.VMEM((2, channels, radii), BF16),
                pltpu.VMEM((members * 2 * channels, 128), F32),
                pltpu.VMEM(coupling.shape, F32),
                pltpu.SMEM(zone.shape, jnp.int32),
                pltpu.SMEM(order.shape, jnp.int32),
                dma((7,)), dma, dma, dma((2,)), dma((2,)), dma((2,)), dma((2,)),
                dma((energies // 2,)), dma((energies // 2,)), dma((energies // 2,)), dma((energies // 2,)),
            ],
            compiler_params=pltpu.CompilerParams(collective_id=0, has_side_effects=True),
        )(green, atoms_last, radial, energy_weight, potential.reshape(folded, 128), coupling, zone, order)
        return both[:folded].reshape(potential.shape), both[folded:].reshape(potential.shape)

    placed = (
        P("energy", "atom", None, None, None),
        P("energy", None, None, None, None),
        P("energy", None, None),
        P("energy"),
        P("atom", None, None),
        P(),
        P("atom", None),
        P(),
    )
    return jax.shard_map(
        body,
        mesh=mesh,
        in_specs=placed,
        out_specs=(P("atom", None, None), P("atom", None, None)),
        check_vma=False,
    )
```
